256 devices in a mesh: rep: 32 (over x_lo, z, core), row: 4 (over y), col: 2 (over x_hi).
Axes of the slice: x: 4 (x_hi: 2, x_lo: 2; x = x_hi * 2 + x_lo), y: 4, z: 8, core: 2. Of those that a mesh axis runs over, the one named last changes fastest.
Arguments:
- weights: bfloat16 [32, 4096, 2048], P('rep', 'row', 'col'), may hold values from -3 to 3
- tracker: bfloat16 [32, 4096, 2048], P('rep', 'row', 'col'), may hold values from -6 to 6
- grad_prev: bfloat16 [32, 4096, 2048], P('rep', 'row', 'col'), may hold values from -6 to 6
- pool: bfloat16 [32, 1024, 2048], P('rep', 'row', 'col'), may hold values from -6 to 6
- out_grads: bfloat16 [32, 2, 512, 4096], P('rep', None, 'col', 'row'), may hold values from -0.25 to 0.25
- row_ids: int32 [32, 2, 512], P('rep'), may hold values from 0 to 1023
- step_index: int32 [1], replicated, may hold values from 0 to 999
Outputs:
- new_weights: bfloat16 [32, 4096, 2048], P('rep', 'row', 'col')
- new_tracker: bfloat16 [32, 4096, 2048], P('rep', 'row', 'col')
The draws below stay inside these ranges and needn't reach their ends.
Inputs may be any that keep to these rules, and one draw needn't show every extreme that they name: `row_ids`: rows may repeat and need not all be used.
All inputs are finite; a program needn't handle non-finite values.
Results may differ from the reference program's by a relative error of at most 0.0085.
Values may be sent and summed in bfloat16 or wider, within the bound.
A program may use at most 128 MiB of HBM per device.

```python
import math
import jax
import jax.numpy as jnp
from jax import lax

D = 2048
QOUT = 4096
GRID = 4
NS_ITERS = 2
STEPS = 2
REPS = 32
BATCH = 512
POOL = 1024


def plant(drawn, own_key, smallest, largest):
    place = [jax.random.randint(jax.random.fold_in(own_key, axis), (), 0, length) for axis, length in enumerate(drawn.shape)]
    longest = drawn.shape.index(max(drawn.shape))
    next_to = place[:longest] + [(place[longest] + 1) % drawn.shape[longest]] + place[longest + 1:]
    return drawn.at[tuple(place)].set(smallest).at[tuple(next_to)].set(largest)


def block_scale(key, dims, shards, low, top_value):
    gain = 1.0
    for dim, parts in shards:
        draws = jax.random.uniform(jax.random.fold_in(jax.random.fold_in(key, 6), dim), (parts,), jnp.float32, low / len(shards), top_value / len(shards))
        gain = gain * jnp.repeat(jnp.exp(draws), dims[dim] // parts).reshape((-1,) + (1,) * (len(dims) - 1 - dim))
    return gain


def centred(key, shape, deviation, reach, cuts=(), kind=jnp.bfloat16):
    factor_of = block_scale(key, shape, cuts, -0.22, 0.18) if cuts else 1.0
    drawn = jax.random.normal(key, shape, jnp.float32) * deviation * factor_of
    return jnp.minimum(jnp.maximum(drawn, -reach), reach).astype(kind)


def setup_inputs(seed: int = 0) -> dict:
    seeds = jax.random.split(jax.random.key(seed), 8)
    return {
        "weights": centred(seeds[0], (REPS, QOUT, D), 0.5, 3.0, ((0, 32), (1, 4), (2, 2))),
        "tracker": centred(seeds[1], (REPS, QOUT, D), 1.0, 6.0, ((0, 32), (1, 4), (2, 2))),
        "grad_prev": centred(seeds[2], (REPS, QOUT, D), 1.0, 6.0, ((0, 32), (1, 4), (2, 2))),
        "pool": centred(seeds[3], (REPS, POOL, D), 1.0, 6.0, ((0, 32), (1, 4), (2, 2))),
        "out_grads": centred(seeds[4], (REPS, STEPS, BATCH, QOUT), BATCH ** -0.5, 0.25, ((0, 32), (2, 2), (3, 4))),
        "row_ids": plant(jax.random.randint(seeds[5], (REPS, STEPS, BATCH), 0, POOL), jax.random.fold_in(seeds[5], 1), 0, POOL - 1).astype(jnp.int32),
        "step_index": jax.random.randint(seeds[6], (1,), 0, 1000).astype(jnp.int32),
    }


quintic_a = 3.4445
quintic_b = -4.775
quintic_c = 2.0315

def orthogonalize(block):
    norm = jnp.sqrt(jnp.sum(block * block)) + 1e-07
    iterate = (block / norm).astype(jnp.bfloat16)
    for turn in range(NS_ITERS):
        gram = jnp.dot(iterate.T, iterate, preferred_element_type=jnp.float32).astype(jnp.bfloat16)
        square = jnp.dot(gram, gram, preferred_element_type=jnp.float32)
        poly = (quintic_b * gram.astype(jnp.float32) + quintic_c * square).astype(jnp.bfloat16)
        iterate = (quintic_a * iterate.astype(jnp.float32) + jnp.dot(iterate, poly, preferred_element_type=jnp.float32)).astype(jnp.bfloat16)
    return iterate

def block_view(matrix):
    shaped = matrix.reshape(GRID, QOUT // GRID, GRID, D // GRID).transpose(0, 2, 1, 3)
    return shaped.reshape(GRID * GRID, QOUT // GRID, D // GRID)

def matrix_view(blocks):
    shaped = blocks.reshape(GRID, GRID, QOUT // GRID, D // GRID).transpose(0, 2, 1, 3)
    return shaped.reshape(QOUT, D)

def gradient(pool_rows, out_grad, chosen_ids):
    chosen = jnp.take(pool_rows, chosen_ids.astype(jnp.int32), axis=0)
    return jnp.dot(out_grad.T, chosen, preferred_element_type=jnp.float32)

def reference(weights, tracker, grad_prev, pool, out_grads, row_ids, step_index):
    levels = REPS.bit_length() - 1
    replica = jnp.arange(REPS, dtype=jnp.int32)
    scale = 0.2 * math.sqrt(QOUT // GRID)
    for step in range(STEPS):
        bit = ((step_index[0] + step) % levels).astype(jnp.int32)
        partner = jnp.bitwise_xor(replica, jnp.left_shift(jnp.ones((), jnp.int32), bit))

        def one(index):
            other = partner[index]
            fresh = gradient(pool[index], out_grads[index, step], row_ids[index, step])
            if step == 0:
                older = grad_prev[index].astype(jnp.float32)
            else:
                older = gradient(pool[index], out_grads[index, step - 1], row_ids[index, step - 1])
            mixed = (0.5 * (tracker[index].astype(jnp.float32) + tracker[other].astype(jnp.float32)) + fresh - older).astype(jnp.bfloat16)
            update = matrix_view(lax.map(orthogonalize, block_view(mixed.astype(jnp.float32))))
            moved = 0.5 * (weights[index].astype(jnp.float32) + weights[other].astype(jnp.float32)) - scale * update.astype(jnp.float32)
            return (moved.astype(jnp.bfloat16), mixed)
        weights, tracker = lax.map(one, replica)
    return (weights, tracker)
```

```python
import functools
import math

import jax
import jax.numpy as jnp
from jax import lax
from jax.experimental import pallas as pl
from jax.experimental.pallas import tpu as pltpu
from jax.sharding import PartitionSpec as P

MESH = pl.DeviceIdType.MESH
BLOCK = 512
TILE = 256
NS_ITERS = 2

quintic_a = 3.4445
quintic_b = -4.775
quintic_c = 2.0315


def flipped(index, bit):
    step = 1 << bit
    return index + step * (1 - 2 * ((index // step) % 2))


def transposed_dot(a, b):
    return lax.dot_general(a, b, (((0,), (0,)), ((), ())), preferred_element_type=jnp.float32)


def kernel(
    first, second, outer, inner,
    ids, weights, tracker, grad_prev, pool, og,
    new_w, new_t,
    t_own, t_in, g_own, y0, yb, pool_all, og_all, chosen, delta, acc, x_ref, poly,
    w_own, w_in, w_half, w_in2, w_all,
    lsem, psend, precv, osend, orecv, tsend, trecv, ysend, yrecv, wsend, wrecv,
):
    rep, row, col = lax.axis_index("rep"), lax.axis_index("row"), lax.axis_index("col")
    rows = lax.axis_size("row")
    right, left = {"row": (row + 1) % rows}, {"row": (row + rows - 1) % rows}
    across = {"col": 1 - col}
    to_first, to_second = {"rep": flipped(rep, first)}, {"rep": flipped(rep, second)}
    to_outer, to_inner = {"rep": flipped(rep, outer)}, {"rep": flipped(rep, inner)}
    half = (rep // (1 << outer)) % 2

    barrier = pltpu.get_barrier_semaphore()
    for peer in (right, left, across, to_first, to_second):
        pl.semaphore_signal(barrier, inc=1, device_id=peer, device_id_type=MESH)
    pl.semaphore_wait(barrier, 5)

    def remote(src, dst, send, recv, peer):
        return pltpu.make_async_remote_copy(
            src_ref=src, dst_ref=dst, send_sem=send, recv_sem=recv,
            device_id=peer, device_id_type=MESH,
        )

    def pool_rows(owner, start=0, size=256):
        return pool_all.at[pl.ds(pl.multiple_of(owner * 256 + start, 128), size), :]

    def columns(c):
        return pl.ds(pl.multiple_of(c * BLOCK, BLOCK), BLOCK)

    def og_part(step, owner):
        return og_all.at[step, pl.ds(pl.multiple_of(owner * 256, 256), 256), :]

    def w_rows(which):
        return pl.ds(pl.multiple_of(which * 512, 512), 512)

    to_right = remote(pool, pool_rows(row), psend.at[0], precv.at[0], right)
    to_left = remote(pool, pool_rows(row), psend.at[1], precv.at[1], left)
    to_right.start()
    to_left.start()
    og_copies = [
        remote(og.at[step], og_part(step, col), osend.at[step], orecv.at[step], across)
        for step in range(2)
    ]
    og_copies[0].start()

    def t_copy(c):
        return remote(tracker.at[:, columns(c)], t_in.at[c], tsend.at[c], trecv.at[c], to_first)

    w_out = remote(weights.at[w_rows(1 - half), :], w_in, wsend.at[0], wrecv.at[0], to_outer)
    w_mid = remote(w_half, w_in2, wsend.at[1], wrecv.at[1], to_inner)
    w_back = remote(
        w_all.at[w_rows(half), :], w_all.at[w_rows(half), :], wsend.at[2], wrecv.at[2], to_outer
    )
    t_copy(0).start()
    t_copy(1).start()
    w_out.start()
    og_copies[1].start()

    local = [
        pltpu.make_async_copy(weights.at[w_rows(half), :], w_own, lsem.at[0]),
        pltpu.make_async_copy(pool, pool_rows(row), lsem.at[1]),
        pltpu.make_async_copy(og.at[0], og_part(0, col), lsem.at[2]),
        pltpu.make_async_copy(og.at[1], og_part(1, col), lsem.at[3]),
        pltpu.make_async_copy(tracker.at[:, pl.ds(0, BLOCK)], t_own.at[0], lsem.at[4]),
        pltpu.make_async_copy(tracker.at[:, pl.ds(BLOCK, BLOCK)], t_own.at[1], lsem.at[5]),
        pltpu.make_async_copy(grad_prev.at[:, pl.ds(0, BLOCK)], g_own.at[0], lsem.at[6]),
        pltpu.make_async_copy(grad_prev.at[:, pl.ds(BLOCK, BLOCK)], g_own.at[1], lsem.at[7]),
    ]
    for copy in local:
        copy.start()
    for copy in local:
        copy.wait()

    def average_outer():
        w_out.wait()

        @pl.loop(0, 512 // TILE)
        def _(i):
            at = pl.ds(pl.multiple_of(i * TILE, TILE), TILE)
            w_half[at, :] = (
                0.5 * (w_own[at, :].astype(jnp.float32) + w_in[at, :].astype(jnp.float32))
            ).astype(jnp.bfloat16)

        w_mid.start()

    def average_inner():
        w_mid.wait()

        @pl.loop(0, 512 // TILE)
        def _(i):
            at = pl.ds(pl.multiple_of(i * TILE, TILE), TILE)
            to = pl.ds(pl.multiple_of(half * 512 + i * TILE, TILE), TILE)
            w_all[to, :] = (
                0.5 * (w_half[at, :].astype(jnp.float32) + w_in2[at, :].astype(jnp.float32))
            ).astype(jnp.bfloat16)

        w_back.start()

    if outer == 0:
        average_outer()

    on_left, on_right = (row + rows - 1) % rows, (row + 1) % rows
    to_right.wait()
    pass_right = remote(
        pool_rows(on_left, 0, 128), pool_rows(on_left, 0, 128), psend.at[2], precv.at[2], right
    )
    pass_right.start()
    to_left.wait()
    pass_left = remote(
        pool_rows(on_right, 128, 128), pool_rows(on_right, 128, 128), psend.at[3], precv.at[3], left
    )
    pass_left.start()
    pass_right.wait()
    pass_left.wait()

    @pl.loop(0, 4)
    def _(i):
        at = pl.ds(pl.multiple_of(i * TILE, TILE), TILE)
        places = lax.broadcasted_iota(jnp.int32, (TILE, 1024), 1)
        picks = (ids[at, :] == places).astype(jnp.bfloat16)
        chosen[at, :] = jnp.dot(
            picks, pool_all[...], preferred_element_type=jnp.float32
        ).astype(jnp.bfloat16)

    og_copies[0].wait()

    @pl.loop(0, 2)
    def _(c):
        t_copy(c).wait()

        @pl.loop(0, 4)
        def _(i):
            at = pl.ds(pl.multiple_of(i * TILE, TILE), TILE)
            fresh = transposed_dot(og_all[0, :, at], chosen[pl.ds(0, 512), columns(c)])
            mixed = (
                0.5 * (t_own[c, at, :].astype(jnp.float32) + t_in[c, at, :].astype(jnp.float32))
                + fresh
                - g_own[c, at, :].astype(jnp.float32)
            )
            y0[c, at, :] = mixed.astype(jnp.bfloat16)
            delta[c, at, :] = fresh

        remote(y0.at[c], yb.at[0, c], ysend.at[c], yrecv.at[c], to_second).start()

    if outer != 0:
        average_outer()
    og_copies[1].wait()

    @pl.loop(0, 2)
    def _(c):
        @pl.loop(0, 4)
        def _(i):
            at = pl.ds(pl.multiple_of(i * TILE, TILE), TILE)
            fresh = transposed_dot(og_all[1, :, at], chosen[pl.ds(512, 512), columns(c)])
            delta[c, at, :] = fresh - delta[c, at, :]

    def orthogonalize(block, c, share):
        def squares(i, total):
            at = pl.ds(pl.multiple_of(i * TILE, TILE), TILE)
            values = block[at, :].astype(jnp.float32)
            return total + jnp.sum(values * values, axis=0, keepdims=True)

        total = lax.fori_loop(0, 4, squares, jnp.zeros((1, BLOCK), jnp.float32))
        inverse = 1.0 / (jnp.sqrt(jnp.sum(total, axis=1, keepdims=True)) + 1e-07)

        @pl.loop(0, 4)
        def _(i):
            at = pl.ds(pl.multiple_of(i * TILE, TILE), TILE)
            x_ref[at, :] = (block[at, :].astype(jnp.float32) * inverse).astype(jnp.bfloat16)

        @pl.loop(0, NS_ITERS)
        def _(turn):
            x = x_ref[...]
            gram = transposed_dot(x, x).astype(jnp.bfloat16)
            square = jnp.dot(gram, gram, preferred_element_type=jnp.float32)
            poly[...] = (quintic_b * gram.astype(jnp.float32) + quintic_c * square).astype(
                jnp.bfloat16
            )

            @pl.loop(0, 4)
            def _(i):
                at = pl.ds(pl.multiple_of(i * TILE, TILE), TILE)
                tile = x_ref[at, :]
                x_ref[at, :] = (
                    quintic_a * tile.astype(jnp.float32)
                    + jnp.dot(tile, poly[...], preferred_element_type=jnp.float32)
                ).astype(jnp.bfloat16)

        @pl.loop(0, 4)
        def _(i):
            at = pl.ds(pl.multiple_of(i * TILE, TILE), TILE)
            acc[c, at, :] += share * x_ref[at, :].astype(jnp.float32)

    acc[...] = jnp.zeros_like(acc)

    @pl.loop(0, 2)
    def _(c):
        orthogonalize(y0.at[c], c, 0.5)

    average_inner()

    @pl.loop(0, 2)
    def _(c):
        remote(y0.at[c], yb.at[0, c], ysend.at[c], yrecv.at[c], to_second).wait()

        @pl.loop(0, 4)
        def _(i):
            at = pl.ds(pl.multiple_of(i * TILE, TILE), TILE)
            mixed = (
                0.5 * (y0[c, at, :].astype(jnp.float32) + yb[0, c, at, :].astype(jnp.float32))
                + delta[c, at, :]
            ).astype(jnp.bfloat16)
            yb[1, c, at, :] = mixed
            new_t[at, columns(c)] = mixed

        @pl.loop(0, 2)
        def _(k):
            orthogonalize(yb.at[k, c], c, 0.5 + 0.5 * k.astype(jnp.float32))

    w_back.wait()
    scale = 0.2 * math.sqrt(1024)

    @pl.loop(0, 2)
    def _(c):
        @pl.loop(0, 4)
        def _(i):
            at = pl.ds(pl.multiple_of(i * TILE, TILE), TILE)
            new_w[at, columns(c)] = (
                w_all[at, columns(c)].astype(jnp.float32) - scale * acc[c, at, :]
            ).astype(jnp.bfloat16)


COST = (0, 1, 2, 4, 1)


def both_steps(first, levels, ids, weights, tracker, grad_prev, pool, og):
    second = (first + 1) % levels
    outer, inner = (first, second) if COST[first] <= COST[second] else (second, first)
    anywhere = pl.BlockSpec(memory_space=pl.ANY)
    vmem = pl.BlockSpec(memory_space=pltpu.VMEM)
    bf16, f32 = jnp.bfloat16, jnp.float32
    dma = pltpu.SemaphoreType.DMA
    return pl.pallas_call(
        functools.partial(kernel, first, second, outer, inner),
        out_shape=(jax.ShapeDtypeStruct((1024, 1024), bf16),) * 2,
        in_specs=[vmem] + [anywhere] * 5,
        out_specs=(vmem, vmem),
        scratch_shapes=[
            pltpu.VMEM((2, 1024, BLOCK), bf16),
            pltpu.VMEM((2, 1024, BLOCK), bf16),
            pltpu.VMEM((2, 1024, BLOCK), bf16),
            pltpu.VMEM((2, 1024, BLOCK), bf16),
            pltpu.VMEM((2, 2, 1024, BLOCK), bf16),
            pltpu.VMEM((1024, 1024), bf16),
            pltpu.VMEM((2, 512, 1024), bf16),
            pltpu.VMEM((1024, 1024), bf16),
            pltpu.VMEM((2, 1024, BLOCK), f32),
            pltpu.VMEM((2, 1024, BLOCK), f32),
            pltpu.VMEM((1024, BLOCK), bf16),
            pltpu.VMEM((BLOCK, BLOCK), bf16),
            pltpu.VMEM((512, 1024), bf16),
            pltpu.VMEM((512, 1024), bf16),
            pltpu.VMEM((512, 1024), bf16),
            pltpu.VMEM((512, 1024), bf16),
            pltpu.VMEM((1024, 1024), bf16),
            dma((8,)), dma((4,)), dma((4,)), dma((2,)), dma((2,)),
            dma((2,)), dma((2,)), dma((2,)), dma((2,)), dma((3,)), dma((3,)),
        ],
        compiler_params=pltpu.CompilerParams(
            collective_id=first, has_side_effects=True, vmem_limit_bytes=58 << 20
        ),
        name=f"steps_{first}",
    )(ids, weights, tracker, grad_prev, pool, og)


def body(weights, tracker, grad_prev, pool, out_grads, row_ids, step_index):
    levels = lax.axis_size("rep").bit_length() - 1
    branches = [functools.partial(both_steps, first, levels) for first in range(levels)]
    new_w, new_t = lax.switch(
        step_index[0] % levels,
        branches,
        row_ids.reshape(1024, 1),
        weights[0],
        tracker[0],
        grad_prev[0],
        pool[0],
        out_grads[0],
    )
    return (new_w[None], new_t[None])


def solution(mesh):
    in_specs = (
        P("rep", "row", "col"),
        P("rep", "row", "col"),
        P("rep", "row", "col"),
        P("rep", "row", "col"),
        P("rep", None, "col", "row"),
        P("rep", None, None),
        P(),
    )
    out_specs = (P("rep", "row", "col"), P("rep", "row", "col"))
    return jax.shard_map(body, mesh=mesh, in_specs=in_specs, out_specs=out_specs, check_vma=False)
```

```python
import functools
import math

import jax
import jax.numpy as jnp
from jax import lax
from jax.experimental import pallas as pl
from jax.experimental.pallas import tpu as pltpu
from jax.sharding import PartitionSpec as P

MESH = pl.DeviceIdType.MESH
BLOCK = 512
TILE = 256
NS_ITERS = 2

quintic_a = 3.4445
quintic_b = -4.775
quintic_c = 2.0315


def flipped(index, bit):
    step = 1 << bit
    return index + step * (1 - 2 * ((index // step) % 2))


def transposed_dot(a, b):
    return lax.dot_general(a, b, (((0,), (0,)), ((), ())), preferred_element_type=jnp.float32)


def kernel(
    first, second, outer, inner, ring,
    ids, weights, tracker, grad_prev, pool, og,
    new_w, new_t,
    t_own, t_in, g_own, y0, yb, pool_all, og_all, chosen, delta, acc, x_ref, poly,
    w_own, w_in, w_half, w_in2, w_all, ring_in, ring_sum,
    lsem, psend, precv, osend, orecv, tsend, trecv, ysend, yrecv, wsend, wrecv, rsend, rrecv,
):
    rep, row, col = lax.axis_index("rep"), lax.axis_index("row"), lax.axis_index("col")
    rows = lax.axis_size("row")
    right, left = {"row": (row + 1) % rows}, {"row": (row + rows - 1) % rows}
    across = {"col": 1 - col}
    to_first, to_second = {"rep": flipped(rep, first)}, {"rep": flipped(rep, second)}
    to_outer, to_inner = {"rep": flipped(rep, outer)}, {"rep": flipped(rep, inner)}
    half = (rep // (1 << outer)) % 2
    stride = 1 << first
    place = (rep // stride) % 4
    round_ring = (
        {"rep": rep + stride * ((place + 1) % 4 - place)},
        {"rep": rep + stride * ((place + 3) % 4 - place)},
    )

    peers = [right, left, across, to_first, to_second]
    if ring:
        peers += round_ring
    barrier = pltpu.get_barrier_semaphore()
    for peer in peers:
        pl.semaphore_signal(barrier, inc=1, device_id=peer, device_id_type=MESH)
    pl.semaphore_wait(barrier, len(peers))

    def remote(src, dst, send, recv, peer):
        return pltpu.make_async_remote_copy(
            src_ref=src, dst_ref=dst, send_sem=send, recv_sem=recv,
            device_id=peer, device_id_type=MESH,
        )

    def pool_rows(owner, start=0, size=256):
        return pool_all.at[pl.ds(pl.multiple_of(owner * 256 + start, 128), size), :]

    def columns(c):
        return pl.ds(c * BLOCK, BLOCK)

    def og_part(step, owner):
        return og_all.at[step, pl.ds(pl.multiple_of(owner * 256, 256), 256), :]

    def w_rows(which, piece=0, size=512):
        return pl.ds(pl.multiple_of(which * 512 + piece * 256, 256), size)

    def tiles(count=4):
        return [pl.ds(i * TILE, TILE) for i in range(count)]

    to_right = remote(pool, pool_rows(row), psend.at[0], precv.at[0], right)
    to_left = remote(pool, pool_rows(row), psend.at[1], precv.at[1], left)
    to_right.start()
    to_left.start()
    og_copies = [
        remote(og.at[step], og_part(step, col), osend.at[step], orecv.at[step], across)
        for step in range(2)
    ]
    og_copies[0].start()

    t_copies = [
        remote(tracker.at[:, columns(c)], t_in.at[c], tsend.at[c], trecv.at[c], to_first)
        for c in range(2)
    ]
    y_copies = [
        remote(y0.at[c], yb.at[0, c], ysend.at[c], yrecv.at[c], to_second) for c in range(2)
    ]
    if not ring:
        w_out = remote(weights.at[w_rows(1 - half), :], w_in, wsend.at[0], wrecv.at[0], to_outer)
        w_mid = [
            remote(
                w_half.at[pl.ds(256 * p, 256), :], w_in2.at[pl.ds(256 * p, 256), :],
                wsend.at[1 + p], wrecv.at[1 + p], to_inner,
            )
            for p in range(2)
        ]
        w_back = [
            remote(
                w_all.at[w_rows(half, p, 256), :], w_all.at[w_rows(half, p, 256), :],
                wsend.at[3 + p], wrecv.at[3 + p], to_outer,
            )
            for p in range(2)
        ]

    weights_first = not ring and outer == 1
    if weights_first:
        w_out.start()
    t_copies[0].start()
    t_copies[1].start()
    if not ring and not weights_first:
        w_out.start()
    og_copies[1].start()

    own_rows = pl.ds(0, 1024) if ring else w_rows(half)
    to_rows = pl.ds(0, 1024) if ring else pl.ds(0, 512)
    local = [
        pltpu.make_async_copy(weights.at[own_rows, :], w_own.at[to_rows, :], lsem.at[0]),
        pltpu.make_async_copy(pool, pool_rows(row), lsem.at[1]),
        pltpu.make_async_copy(og.at[0], og_part(0, col), lsem.at[2]),
        pltpu.make_async_copy(og.at[1], og_part(1, col), lsem.at[3]),
        pltpu.make_async_copy(tracker.at[:, columns(0)], t_own.at[0], lsem.at[4]),
        pltpu.make_async_copy(tracker.at[:, columns(1)], t_own.at[1], lsem.at[5]),
        pltpu.make_async_copy(grad_prev.at[:, columns(0)], g_own.at[0], lsem.at[6]),
        pltpu.make_async_copy(grad_prev.at[:, columns(1)], g_own.at[1], lsem.at[7]),
    ]
    for copy in local:
        copy.start()
    for copy in local:
        copy.wait()

    def average_outer():
        if ring:
            return
        w_out.wait()
        for p in range(2):
            at = pl.ds(256 * p, 256)
            w_half[at, :] = (
                0.5 * (w_own[at, :].astype(jnp.float32) + w_in[at, :].astype(jnp.float32))
            ).astype(jnp.bfloat16)

    def send_middle():
        if not ring:
            for copy in w_mid:
                copy.start()

    def average_inner():
        if ring:
            return
        for p in range(2):
            w_mid[p].wait()
            at = pl.ds(256 * p, 256)
            w_all[w_rows(half, p, 256), :] = (
                0.5 * (w_half[at, :].astype(jnp.float32) + w_in2[at, :].astype(jnp.float32))
            ).astype(jnp.bfloat16)
            w_back[p].start()

    def ring_rows(way, ahead):
        return pl.ds(pl.multiple_of(512 * way + 128 * ((place + ahead + 4) % 4), 128), 128)

    def ring_copy(way, hop):
        sign = 1 - 2 * way
        if hop < 3:
            src = w_own.at[ring_rows(way, 0), :] if hop == 0 else ring_sum.at[way, hop - 1]
            dst = ring_in.at[way, hop]
        else:
            src = dst = w_all.at[ring_rows(way, sign * (4 - hop)), :]
        at = way * 6 + hop
        return remote(src, dst, rsend.at[at], rrecv.at[at], round_ring[way])

    def ring_advance(hop):
        if not ring:
            return
        for way in range(2):
            if hop > 0:
                ring_copy(way, hop - 1).wait()
            if 1 <= hop <= 3:
                at = ring_rows(way, (2 * way - 1) * hop)
                total = w_own[at, :].astype(jnp.float32) + ring_in[way, hop - 1].astype(
                    jnp.float32
                )
                if hop < 3:
                    ring_sum[way, hop - 1] = total.astype(jnp.bfloat16)
                else:
                    w_all[at, :] = (0.25 * total).astype(jnp.bfloat16)
            if hop < 6:
                ring_copy(way, hop).start()

    ring_advance(0)
    if outer == 0:
        average_outer()
        send_middle()

    on_left, on_right = (row + rows - 1) % rows, (row + 1) % rows
    to_right.wait()
    pass_right = remote(
        pool_rows(on_left, 0, 128), pool_rows(on_left, 0, 128), psend.at[2], precv.at[2], right
    )
    pass_right.start()
    to_left.wait()
    pass_left = remote(
        pool_rows(on_right, 128, 128), pool_rows(on_right, 128, 128), psend.at[3], precv.at[3], left
    )
    pass_left.start()
    pass_right.wait()
    pass_left.wait()

    for step in range(2):
        for i in range(2):
            places = lax.broadcasted_iota(jnp.int32, (1024, TILE), 0)
            picks = jnp.where(
                ids[step : step + 1, pl.ds(i * TILE, TILE)] == places, 1.0, 0.0
            ).astype(jnp.bfloat16)
            chosen[pl.ds(step * 512 + i * TILE, TILE), :] = transposed_dot(
                picks, pool_all[...]
            ).astype(jnp.bfloat16)

    ring_advance(1)
    if weights_first:
        average_outer()
        send_middle()
    og_copies[0].wait()

    for c in range(2):
        t_copies[c].wait()
        if c == 1 and outer != 0 and not weights_first:
            average_outer()
            send_middle()

        @pl.loop(0, 4)
        def _(i):
            at = pl.ds(pl.multiple_of(i * TILE, TILE), TILE)
            fresh = transposed_dot(og_all[0, :, at], chosen[pl.ds(0, 512), columns(c)])
            mixed = (
                0.5 * (t_own[c, at, :].astype(jnp.float32) + t_in[c, at, :].astype(jnp.float32))
                + fresh
                - g_own[c, at, :].astype(jnp.float32)
            )
            y0[c, at, :] = mixed.astype(jnp.bfloat16)
            delta[c, at, :] = fresh

        y_copies[c].start()
        ring_advance(2 + c)

    og_copies[1].wait()

    @pl.loop(0, 4)
    def _(i):
        at = pl.ds(pl.multiple_of(i * TILE, TILE), TILE)
        for c in range(2):
            fresh = transposed_dot(og_all[1, :, at], chosen[pl.ds(512, 512), columns(c)])
            delta[c, at, :] = fresh - delta[c, at, :]

    def orthogonalize(blocks):
        for k, block in enumerate(blocks):
            total = jnp.zeros((1, BLOCK), jnp.float32)
            for at in tiles():
                values = block[at, :].astype(jnp.float32)
                total = total + jnp.sum(values * values, axis=0, keepdims=True)
            inverse = 1.0 / (jnp.sqrt(jnp.sum(total, axis=1, keepdims=True)) + 1e-07)
            for at in tiles():
                x_ref[k, at, :] = (block[at, :].astype(jnp.float32) * inverse).astype(
                    jnp.bfloat16
                )

        @pl.loop(0, NS_ITERS)
        def _(turn):
            for k in range(2):
                x = x_ref[k]
                gram = transposed_dot(x, x).astype(jnp.bfloat16)
                square = jnp.dot(gram, gram, preferred_element_type=jnp.float32)
                poly[k] = (quintic_b * gram.astype(jnp.float32) + quintic_c * square).astype(
                    jnp.bfloat16
                )
            for k in range(2):
                for at in tiles():
                    tile = x_ref[k, at, :]
                    x_ref[k, at, :] = (
                        quintic_a * tile.astype(jnp.float32)
                        + jnp.dot(tile, poly[k], preferred_element_type=jnp.float32)
                    ).astype(jnp.bfloat16)

    orthogonalize([y0.at[0], y0.at[1]])
    for c in range(2):
        for at in tiles():
            acc[c, at, :] = 0.5 * x_ref[c, at, :].astype(jnp.float32)

    late = inner in (3, 4)
    ring_advance(4)
    if not late:
        average_inner()

    @pl.loop(0, 2)
    def _(c):
        remote(y0.at[c], yb.at[0, c], ysend.at[c], yrecv.at[c], to_second).wait()
        to = pl.ds(pl.multiple_of(c * BLOCK, BLOCK), BLOCK)
        for at in tiles():
            mixed = (
                0.5 * (y0[c, at, :].astype(jnp.float32) + yb[0, c, at, :].astype(jnp.float32))
                + delta[c, at, :]
            ).astype(jnp.bfloat16)
            yb[1, c, at, :] = mixed
            new_t[at, to] = mixed
        orthogonalize([yb.at[0, c], yb.at[1, c]])
        for at in tiles():
            acc[c, at, :] += 0.5 * x_ref[0, at, :].astype(jnp.float32) + x_ref[1, at, :].astype(
                jnp.float32
            )

        if ring:
            @pl.when(c == 0)
            def _():
                ring_advance(5)

    ring_advance(6)
    if not ring:
        if late:
            average_inner()
        for copy in w_back:
            copy.wait()
    scale = 0.2 * math.sqrt(1024)
    for c in range(2):
        for at in tiles():
            new_w[at, columns(c)] = (
                w_all[at, columns(c)].astype(jnp.float32) - scale * acc[c, at, :]
            ).astype(jnp.bfloat16)


COST = (0, 1, 2, 4, 1)


def both_steps(first, levels, ids, weights, tracker, grad_prev, pool, og):
    second = (first + 1) % levels
    outer, inner = (first, second) if COST[first] <= COST[second] else (second, first)
    ring = first == 2
    anywhere = pl.BlockSpec(memory_space=pl.ANY)
    vmem = pl.BlockSpec(memory_space=pltpu.VMEM)
    bf16, f32 = jnp.bfloat16, jnp.float32
    dma = pltpu.SemaphoreType.DMA
    return pl.pallas_call(
        functools.partial(kernel, first, second, outer, inner, ring),
        out_shape=(jax.ShapeDtypeStruct((1024, 1024), bf16),) * 2,
        in_specs=[vmem] + [anywhere] * 5,
        out_specs=(vmem, vmem),
        scratch_shapes=[
            pltpu.VMEM((2, 1024, BLOCK), bf16),
            pltpu.VMEM((2, 1024, BLOCK), bf16),
            pltpu.VMEM((2, 1024, BLOCK), bf16),
            pltpu.VMEM((2, 1024, BLOCK), bf16),
            pltpu.VMEM((2, 2, 1024, BLOCK), bf16),
            pltpu.VMEM((1024, 1024), bf16),
            pltpu.VMEM((2, 512, 1024), bf16),
            pltpu.VMEM((1024, 1024), bf16),
            pltpu.VMEM((2, 1024, BLOCK), f32),
            pltpu.VMEM((2, 1024, BLOCK), f32),
            pltpu.VMEM((2, 1024, BLOCK), bf16),
            pltpu.VMEM((2, BLOCK, BLOCK), bf16),
            pltpu.VMEM((1024 if ring else 512, 1024), bf16),
            pltpu.VMEM((512, 1024), bf16),
            pltpu.VMEM((512, 1024), bf16),
            pltpu.VMEM((512, 1024), bf16),
            pltpu.VMEM((1024, 1024), bf16),
            pltpu.VMEM((2, 3, 128, 1024), bf16),
            pltpu.VMEM((2, 2, 128, 1024), bf16),
            dma((8,)), dma((4,)), dma((4,)), dma((2,)), dma((2,)),
            dma((2,)), dma((2,)), dma((2,)), dma((2,)), dma((5,)), dma((5,)), dma((12,)), dma((12,)),
        ],
        compiler_params=pltpu.CompilerParams(
            collective_id=first, has_side_effects=True, vmem_limit_bytes=58 << 20
        ),
        name=f"steps_{first}",
    )(ids, weights, tracker, grad_prev, pool, og)


def body(weights, tracker, grad_prev, pool, out_grads, row_ids, step_index):
    levels = lax.axis_size("rep").bit_length() - 1
    branches = [functools.partial(both_steps, first, levels) for first in range(levels)]
    new_w, new_t = lax.switch(
        step_index[0] % levels,
        branches,
        row_ids[0],
        weights[0],
        tracker[0],
        grad_prev[0],
        pool[0],
        out_grads[0],
    )
    return (new_w[None], new_t[None])


def solution(mesh):
    in_specs = (
        P("rep", "row", "col"),
        P("rep", "row", "col"),
        P("rep", "row", "col"),
        P("rep", "row", "col"),
        P("rep", None, "col", "row"),
        P("rep", None, None),
        P(),
    )
    out_specs = (P("rep", "row", "col"), P("rep", "row", "col"))
    return jax.shard_map(body, mesh=mesh, in_specs=in_specs, out_specs=out_specs, check_vma=False)
```

```python
import functools
import math

import jax
import jax.numpy as jnp
from jax import lax
from jax.experimental import pallas as pl
from jax.experimental.pallas import tpu as pltpu
from jax.sharding import PartitionSpec as P

MESH = pl.DeviceIdType.MESH
BLOCK = 512
TILE = 256
NS_ITERS = 2

quintic_a = 3.4445
quintic_b = -4.775
quintic_c = 2.0315


def flipped(index, bit):
    step = 1 << bit
    return index + step * (1 - 2 * ((index // step) % 2))


def transposed_dot(a, b):
    return lax.dot_general(a, b, (((0,), (0,)), ((), ())), preferred_element_type=jnp.float32)


def kernel(
    first, second, outer, inner, ring,
    ids, weights, tracker, grad_prev, pool, og,
    new_w, new_t,
    t_own, t_in, g_own, y_all, pool_all, og_all, chosen, delta, acc, x_ref, poly,
    w_own, w_in, w_half, w_in2, w_all, ring_in,
    lsem, psend, precv, osend, orecv, tsend, trecv, ysend, yrecv, wsend, wrecv, rsend, rrecv,
):
    rep, row, col = lax.axis_index("rep"), lax.axis_index("row"), lax.axis_index("col")
    rows = lax.axis_size("row")
    right, left = {"row": (row + 1) % rows}, {"row": (row + rows - 1) % rows}
    across = {"col": 1 - col}
    to_first, to_second = {"rep": flipped(rep, first)}, {"rep": flipped(rep, second)}
    to_outer, to_inner = {"rep": flipped(rep, outer)}, {"rep": flipped(rep, inner)}
    half = (rep // (1 << outer)) % 2
    stride = 1 << first
    place = (rep // stride) % 4
    both = flipped(flipped(rep, first), second)
    group = (to_first, to_second, {"rep": both})
    others = [(peer["rep"] // stride) % 4 for peer in group]

    peers = [right, left, across, to_first, to_second]
    if ring:
        peers.append(group[2])
    barrier = pltpu.get_barrier_semaphore()
    for peer in peers:
        pl.semaphore_signal(barrier, inc=1, device_id=peer, device_id_type=MESH)
    pl.semaphore_wait(barrier, len(peers))

    def remote(src, dst, send, recv, peer):
        return pltpu.make_async_remote_copy(
            src_ref=src, dst_ref=dst, send_sem=send, recv_sem=recv,
            device_id=peer, device_id_type=MESH,
        )

    def pool_rows(owner, start=0, size=256):
        return pool_all.at[pl.ds(pl.multiple_of(owner * 256 + start, 128), size), :]

    def columns(c):
        return pl.ds(pl.multiple_of(c * BLOCK, BLOCK), BLOCK)

    def og_part(step, owner):
        return og_all.at[step, pl.ds(pl.multiple_of(owner * 256, 256), 256), :]

    def w_rows(which, piece=0, size=512):
        return pl.ds(pl.multiple_of(which * 512 + piece * 256, 256), size)

    def each_tile(step):
        @pl.loop(0, 4)
        def _(i):
            step(pl.ds(pl.multiple_of(i * TILE, TILE), TILE))

    to_right = remote(pool, pool_rows(row), psend.at[0], precv.at[0], right)
    to_left = remote(pool, pool_rows(row), psend.at[1], precv.at[1], left)
    to_right.start()
    to_left.start()
    og_copies = [
        remote(og.at[step], og_part(step, col), osend.at[step], orecv.at[step], across)
        for step in range(2)
    ]
    og_copies[0].start()

    def t_copy(c):
        return remote(tracker.at[:, columns(c)], t_in.at[c], tsend.at[c], trecv.at[c], to_first)

    def y_copy(c, part):
        at = pl.ds(pl.multiple_of(part * 512, 512), 512)
        return remote(
            y_all.at[0, c, at, :], y_all.at[1 + c, 0, at, :],
            ysend.at[c, part], yrecv.at[c, part], to_second,
        )

    if not ring:
        w_out = remote(weights.at[w_rows(1 - half), :], w_in, wsend.at[0], wrecv.at[0], to_outer)
        w_mid = [
            remote(
                w_half.at[pl.ds(256 * p, 256), :], w_in2.at[pl.ds(256 * p, 256), :],
                wsend.at[1 + p], wrecv.at[1 + p], to_inner,
            )
            for p in range(2)
        ]
        w_back = [
            remote(
                w_all.at[w_rows(half, p, 256), :], w_all.at[w_rows(half, p, 256), :],
                wsend.at[3 + p], wrecv.at[3 + p], to_outer,
            )
            for p in range(2)
        ]

    def quarter(owner):
        return pl.ds(pl.multiple_of(owner * 256, 256), 256)

    def quarter_in(j):
        return remote(
            weights.at[quarter(others[j]), :], ring_in.at[j], rsend.at[j], rrecv.at[j], group[j]
        )

    def quarter_out(j):
        return remote(
            w_all.at[quarter(place), :], w_all.at[quarter(place), :],
            rsend.at[3 + j], rrecv.at[3 + j], group[j],
        )

    def average_quarter():
        for j in range(3):
            quarter_in(j).wait()
        total = w_own[...].astype(jnp.float32)
        for j in range(3):
            total += ring_in[j].astype(jnp.float32)
        w_all[quarter(place), :] = (0.25 * total).astype(jnp.bfloat16)
        for j in range(3):
            quarter_out(j).start()

    if ring:
        t_copy(0).start()
        t_copy(1).start()
        for j in range(3):
            quarter_in(j).start()
    weights_first = not ring and outer == 1
    if weights_first:
        w_out.start()
    if not weights_first and not ring:
        t_copy(0).start()
        t_copy(1).start()
    if not ring and not weights_first:
        w_out.start()
    og_copies[1].start()

    own_rows = quarter(place) if ring else w_rows(half)
    local = [
        pltpu.make_async_copy(weights.at[own_rows, :], w_own, lsem.at[0]),
        pltpu.make_async_copy(pool, pool_rows(row), lsem.at[1]),
        pltpu.make_async_copy(og.at[0], og_part(0, col), lsem.at[2]),
        pltpu.make_async_copy(og.at[1], og_part(1, col), lsem.at[3]),
        pltpu.make_async_copy(tracker.at[:, columns(0)], t_own.at[0], lsem.at[4]),
        pltpu.make_async_copy(tracker.at[:, columns(1)], t_own.at[1], lsem.at[5]),
        pltpu.make_async_copy(grad_prev.at[:, columns(0)], g_own.at[0], lsem.at[6]),
        pltpu.make_async_copy(grad_prev.at[:, columns(1)], g_own.at[1], lsem.at[7]),
    ]
    for copy in local:
        copy.start()
    for copy in local:
        copy.wait()

    def average_outer():
        if ring:
            return
        w_out.wait()
        for p in range(2):
            at = pl.ds(256 * p, 256)
            w_half[at, :] = (
                0.5 * (w_own[at, :].astype(jnp.float32) + w_in[at, :].astype(jnp.float32))
            ).astype(jnp.bfloat16)

    def send_middle():
        if not ring:
            for copy in w_mid:
                copy.start()

    def average_inner():
        if ring:
            return
        for p in range(2):
            w_mid[p].wait()
            at = pl.ds(256 * p, 256)
            w_all[w_rows(half, p, 256), :] = (
                0.5 * (w_half[at, :].astype(jnp.float32) + w_in2[at, :].astype(jnp.float32))
            ).astype(jnp.bfloat16)
            w_back[p].start()

    if outer == 0:
        average_outer()
        send_middle()

    on_left, on_right = (row + rows - 1) % rows, (row + 1) % rows
    to_right.wait()
    pass_right = remote(
        pool_rows(on_left, 0, 128), pool_rows(on_left, 0, 128), psend.at[2], precv.at[2], right
    )
    pass_right.start()
    to_left.wait()
    pass_left = remote(
        pool_rows(on_right, 128, 128), pool_rows(on_right, 128, 128), psend.at[3], precv.at[3], left
    )
    pass_left.start()
    if weights_first:
        average_outer()
        t_copy(0).start()
        send_middle()
        t_copy(1).start()
    pass_right.wait()
    pass_left.wait()

    def choose(step):
        @pl.loop(0, 2)
        def _(i):
            places = lax.broadcasted_iota(jnp.int32, (1024, TILE), 0)
            wanted = ids[step : step + 1, pl.ds(pl.multiple_of(i * TILE, TILE), TILE)]
            picks = jnp.where(wanted == places, 1.0, 0.0).astype(jnp.bfloat16)
            chosen[pl.ds(pl.multiple_of(step * 512 + i * TILE, TILE), TILE), :] = transposed_dot(
                picks, pool_all[...]
            ).astype(jnp.bfloat16)

    choose(0)
    og_copies[0].wait()

    @pl.loop(0, 2)
    def _(c):
        t_copy(c).wait()

        if not ring and outer != 0 and not weights_first:
            @pl.when(c == 1)
            def _():
                average_outer()
                send_middle()

        @pl.loop(0, 2)
        def _(part):
            @pl.loop(0, 2)
            def _(i):
                at = pl.ds(pl.multiple_of(part * 512 + i * TILE, TILE), TILE)
                fresh = transposed_dot(og_all[0, :, at], chosen[pl.ds(0, 512), columns(c)])
                mixed = (
                    0.5
                    * (t_own[c, at, :].astype(jnp.float32) + t_in[c, at, :].astype(jnp.float32))
                    + fresh
                    - g_own[c, at, :].astype(jnp.float32)
                )
                y_all[0, c, at, :] = mixed.astype(jnp.bfloat16)
                delta[c, at, :] = fresh

            y_copy(c, part).start()

        if ring:
            @pl.when(c == 1)
            def _():
                average_quarter()

    choose(1)
    og_copies[1].wait()

    @each_tile
    def _(at):
        for c in range(2):
            fresh = transposed_dot(og_all[1, :, at], chosen[pl.ds(512, 512), columns(c)])
            delta[c, at, :] = fresh - delta[c, at, :]

    late = inner in (3, 4)

    @pl.loop(0, 3)
    def _(job):
        c = (job + 1) % 2

        if not ring and not late:
            @pl.when(job == 1)
            def _():
                average_inner()

        @pl.when(job > 0)
        def _():
            y_copy(c, 0).wait()
            y_copy(c, 1).wait()

            @each_tile
            def _(at):
                mixed = (
                    0.5
                    * (
                        y_all[0, c, at, :].astype(jnp.float32)
                        + y_all[1 + c, 0, at, :].astype(jnp.float32)
                    )
                    + delta[c, at, :]
                ).astype(jnp.bfloat16)
                y_all[1 + c, 1, at, :] = mixed
                new_t[at, columns(c)] = mixed

        def squares(i, totals):
            at = pl.ds(pl.multiple_of(i * TILE, TILE), TILE)
            out = []
            for k in range(2):
                values = y_all[job, k, at, :].astype(jnp.float32)
                out.append(totals[k] + jnp.sum(values * values, axis=0, keepdims=True))
            return tuple(out)

        totals = lax.fori_loop(0, 4, squares, (jnp.zeros((1, BLOCK), jnp.float32),) * 2)
        inverse = [
            1.0 / (jnp.sqrt(jnp.sum(total, axis=1, keepdims=True)) + 1e-07) for total in totals
        ]

        @each_tile
        def _(at):
            for k in range(2):
                x_ref[k, at, :] = (
                    y_all[job, k, at, :].astype(jnp.float32) * inverse[k]
                ).astype(jnp.bfloat16)

        @pl.loop(0, NS_ITERS)
        def _(turn):
            for k in range(2):
                x = x_ref[k]
                gram = transposed_dot(x, x).astype(jnp.bfloat16)
                square = jnp.dot(gram, gram, preferred_element_type=jnp.float32)
                poly[k] = (quintic_b * gram.astype(jnp.float32) + quintic_c * square).astype(
                    jnp.bfloat16
                )

            @each_tile
            def _(at):
                for k in range(2):
                    tile = x_ref[k, at, :]
                    x_ref[k, at, :] = (
                        quintic_a * tile.astype(jnp.float32)
                        + jnp.dot(tile, poly[k], preferred_element_type=jnp.float32)
                    ).astype(jnp.bfloat16)

        @pl.when(job == 0)
        def _():
            @each_tile
            def _(at):
                for k in range(2):
                    acc[k, at, :] = 0.5 * x_ref[k, at, :].astype(jnp.float32)

        @pl.when(job > 0)
        def _():
            @each_tile
            def _(at):
                acc[c, at, :] += 0.5 * x_ref[0, at, :].astype(jnp.float32) + x_ref[
                    1, at, :
                ].astype(jnp.float32)

    if ring:
        for j in range(3):
            quarter_out(j).wait()
    else:
        if late:
            average_inner()
        for copy in w_back:
            copy.wait()
    scale = 0.2 * math.sqrt(1024)

    @each_tile
    def _(at):
        for c in range(2):
            new_w[at, columns(c)] = (
                w_all[at, columns(c)].astype(jnp.float32) - scale * acc[c, at, :]
            ).astype(jnp.bfloat16)


COST = (0, 1, 2, 4, 1)


def both_steps(first, levels, ids, weights, tracker, grad_prev, pool, og):
    second = (first + 1) % levels
    outer, inner = (first, second) if COST[first] <= COST[second] else (second, first)
    ring = first == 2
    anywhere = pl.BlockSpec(memory_space=pl.ANY)
    vmem = pl.BlockSpec(memory_space=pltpu.VMEM)
    bf16, f32 = jnp.bfloat16, jnp.float32
    dma = pltpu.SemaphoreType.DMA
    return pl.pallas_call(
        functools.partial(kernel, first, second, outer, inner, ring),
        out_shape=(jax.ShapeDtypeStruct((1024, 1024), bf16),) * 2,
        in_specs=[vmem] + [anywhere] * 5,
        out_specs=(vmem, vmem),
        scratch_shapes=[
            pltpu.VMEM((2, 1024, BLOCK), bf16),
            pltpu.VMEM((2, 1024, BLOCK), bf16),
            pltpu.VMEM((2, 1024, BLOCK), bf16),
            pltpu.VMEM((3, 2, 1024, BLOCK), bf16),
            pltpu.VMEM((1024, 1024), bf16),
            pltpu.VMEM((2, 512, 1024), bf16),
            pltpu.VMEM((1024, 1024), bf16),
            pltpu.VMEM((2, 1024, BLOCK), f32),
            pltpu.VMEM((2, 1024, BLOCK), f32),
            pltpu.VMEM((2, 1024, BLOCK), bf16),
            pltpu.VMEM((2, BLOCK, BLOCK), bf16),
            pltpu.VMEM((256 if ring else 512, 1024), bf16),
            pltpu.VMEM((512, 1024), bf16),
            pltpu.VMEM((512, 1024), bf16),
            pltpu.VMEM((512, 1024), bf16),
            pltpu.VMEM((1024, 1024), bf16),
            pltpu.VMEM((3, 256, 1024), bf16),
            dma((8,)), dma((4,)), dma((4,)), dma((2,)), dma((2,)),
            dma((2,)), dma((2,)), dma((2, 2)), dma((2, 2)), dma((5,)), dma((5,)), dma((6,)), dma((6,)),
        ],
        compiler_params=pltpu.CompilerParams(
            collective_id=first, has_side_effects=True, vmem_limit_bytes=58 << 20
        ),
        name=f"steps_{first}",
    )(ids, weights, tracker, grad_prev, pool, og)


def body(weights, tracker, grad_prev, pool, out_grads, row_ids, step_index):
    levels = lax.axis_size("rep").bit_length() - 1
    branches = [functools.partial(both_steps, first, levels) for first in range(levels)]
    new_w, new_t = lax.switch(
        step_index[0] % levels,
        branches,
        row_ids[0],
        weights[0],
        tracker[0],
        grad_prev[0],
        pool[0],
        out_grads[0],
    )
    return (new_w[None], new_t[None])


def solution(mesh):
    in_specs = (
        P("rep", "row", "col"),
        P("rep", "row", "col"),
        P("rep", "row", "col"),
        P("rep", "row", "col"),
        P("rep", None, "col", "row"),
        P("rep", None, None),
        P(),
    )
    out_specs = (P("rep", "row", "col"), P("rep", "row", "col"))
    return jax.shard_map(body, mesh=mesh, in_specs=in_specs, out_specs=out_specs, check_vma=False)
```

```python
import functools
import math

import jax
import jax.numpy as jnp
from jax import lax
from jax.experimental import pallas as pl
from jax.experimental.pallas import tpu as pltpu
from jax.sharding import PartitionSpec as P

MESH = pl.DeviceIdType.MESH
BLOCK = 512
TILE = 256
NS_ITERS = 2

quintic_a = 3.4445
quintic_b = -4.775
quintic_c = 2.0315


def flipped(index, bit):
    step = 1 << bit
    return index + step * (1 - 2 * ((index // step) % 2))


def transposed_dot(a, b):
    return lax.dot_general(a, b, (((0,), (0,)), ((), ())), preferred_element_type=jnp.float32)


def kernel(
    first, second, outer, inner, ring,
    ids, weights, tracker, grad_prev, pool, og,
    new_w, new_t,
    t_own, t_in, g_own, y_all, pool_all, og_all, chosen, delta, acc, x_ref, poly,
    w_own, w_in, w_half, w_in2, w_all, ring_in,
    lsem, psend, precv, osend, orecv, tsend, trecv, ysend, yrecv, wsend, wrecv, rsend, rrecv,
):
    rep, row, col = lax.axis_index("rep"), lax.axis_index("row"), lax.axis_index("col")
    rows = lax.axis_size("row")
    right, left = {"row": (row + 1) % rows}, {"row": (row + rows - 1) % rows}
    across = {"col": 1 - col}
    to_first, to_second = {"rep": flipped(rep, first)}, {"rep": flipped(rep, second)}
    to_outer, to_inner = {"rep": flipped(rep, outer)}, {"rep": flipped(rep, inner)}
    half = (rep // (1 << outer)) % 2
    stride = 1 << first
    place = (rep // stride) % 4
    both = flipped(flipped(rep, first), second)
    group = (to_first, to_second, {"rep": both})
    others = [(peer["rep"] // stride) % 4 for peer in group]

    peers = [right, left, across, to_first, to_second]
    if ring:
        peers.append(group[2])
    barrier = pltpu.get_barrier_semaphore()
    for peer in peers:
        pl.semaphore_signal(barrier, inc=1, device_id=peer, device_id_type=MESH)
    pl.semaphore_wait(barrier, len(peers))

    def remote(src, dst, send, recv, peer):
        return pltpu.make_async_remote_copy(
            src_ref=src, dst_ref=dst, send_sem=send, recv_sem=recv,
            device_id=peer, device_id_type=MESH,
        )

    def pool_rows(owner, start=0, size=256):
        return pool_all.at[pl.ds(pl.multiple_of(owner * 256 + start, 128), size), :]

    def columns(c):
        return pl.ds(pl.multiple_of(c * BLOCK, BLOCK), BLOCK)

    def og_part(step, owner):
        return og_all.at[step, pl.ds(pl.multiple_of(owner * 256, 256), 256), :]

    def w_rows(which, piece=0, size=512):
        return pl.ds(pl.multiple_of(which * 512 + piece * 128, 128), size)

    def each_tile(step):
        @pl.loop(0, 4)
        def _(i):
            step(pl.ds(pl.multiple_of(i * TILE, TILE), TILE))

    to_right = remote(pool, pool_rows(row), psend.at[0], precv.at[0], right)
    to_left = remote(pool, pool_rows(row), psend.at[1], precv.at[1], left)
    to_right.start()
    to_left.start()
    og_copies = [
        remote(og.at[step], og_part(step, col), osend.at[step], orecv.at[step], across)
        for step in range(2)
    ]
    og_copies[0].start()

    def t_copy(c):
        return remote(tracker.at[:, columns(c)], t_in.at[c], tsend.at[c], trecv.at[c], to_first)

    def y_copy(c, part):
        at = pl.ds(pl.multiple_of(part * 512, 512), 512)
        return remote(
            y_all.at[0, c, at, :], y_all.at[1 + c, 0, at, :],
            ysend.at[c, part], yrecv.at[c, part], to_second,
        )

    if not ring:
        w_out = remote(weights.at[w_rows(1 - half), :], w_in, wsend.at[0], wrecv.at[0], to_outer)
        w_mid = [
            remote(
                w_half.at[pl.ds(128 * p, 128), :], w_in2.at[pl.ds(128 * p, 128), :],
                wsend.at[1 + p], wrecv.at[1 + p], to_inner,
            )
            for p in range(4)
        ]
        w_back = [
            remote(
                w_all.at[w_rows(half, p, 128), :], w_all.at[w_rows(half, p, 128), :],
                wsend.at[5 + p], wrecv.at[5 + p], to_outer,
            )
            for p in range(4)
        ]

    def quarter(owner):
        return pl.ds(pl.multiple_of(owner * 256, 256), 256)

    def quarter_in(j):
        return remote(
            weights.at[quarter(others[j]), :], ring_in.at[j], rsend.at[j], rrecv.at[j], group[j]
        )

    def quarter_out(j):
        return remote(
            w_all.at[quarter(place), :], w_all.at[quarter(place), :],
            rsend.at[3 + j], rrecv.at[3 + j], group[j],
        )

    def average_quarter():
        for j in range(3):
            quarter_in(j).wait()
        total = w_own[...].astype(jnp.float32)
        for j in range(3):
            total += ring_in[j].astype(jnp.float32)
        w_all[quarter(place), :] = (0.25 * total).astype(jnp.bfloat16)
        for j in range(3):
            quarter_out(j).start()

    if ring:
        t_copy(0).start()
        t_copy(1).start()
        for j in range(3):
            quarter_in(j).start()
    weights_first = not ring and outer == 1
    if weights_first:
        w_out.start()
    if not weights_first and not ring:
        t_copy(0).start()
        t_copy(1).start()
    if not ring and not weights_first:
        w_out.start()
    og_copies[1].start()

    own_rows = quarter(place) if ring else w_rows(half)
    local = [
        pltpu.make_async_copy(weights.at[own_rows, :], w_own, lsem.at[0]),
        pltpu.make_async_copy(pool, pool_rows(row), lsem.at[1]),
        pltpu.make_async_copy(og.at[0], og_part(0, col), lsem.at[2]),
        pltpu.make_async_copy(og.at[1], og_part(1, col), lsem.at[3]),
        pltpu.make_async_copy(tracker.at[:, columns(0)], t_own.at[0], lsem.at[4]),
        pltpu.make_async_copy(tracker.at[:, columns(1)], t_own.at[1], lsem.at[5]),
        pltpu.make_async_copy(grad_prev.at[:, columns(0)], g_own.at[0], lsem.at[6]),
        pltpu.make_async_copy(grad_prev.at[:, columns(1)], g_own.at[1], lsem.at[7]),
    ]
    for copy in local:
        copy.start()
    for copy in local:
        copy.wait()

    def average_outer():
        if ring:
            return
        w_out.wait()
        for p in range(2):
            at = pl.ds(256 * p, 256)
            w_half[at, :] = (
                0.5 * (w_own[at, :].astype(jnp.float32) + w_in[at, :].astype(jnp.float32))
            ).astype(jnp.bfloat16)

    def send_middle():
        if not ring:
            for copy in w_mid:
                copy.start()

    def average_inner():
        if ring:
            return
        for p in range(4):
            w_mid[p].wait()
            at = pl.ds(128 * p, 128)
            w_all[w_rows(half, p, 128), :] = (
                0.5 * (w_half[at, :].astype(jnp.float32) + w_in2[at, :].astype(jnp.float32))
            ).astype(jnp.bfloat16)
            w_back[p].start()

    if outer == 0:
        average_outer()
        send_middle()

    on_left, on_right = (row + rows - 1) % rows, (row + 1) % rows
    to_right.wait()
    pass_right = remote(
        pool_rows(on_left, 0, 128), pool_rows(on_left, 0, 128), psend.at[2], precv.at[2], right
    )
    pass_right.start()
    to_left.wait()
    pass_left = remote(
        pool_rows(on_right, 128, 128), pool_rows(on_right, 128, 128), psend.at[3], precv.at[3], left
    )
    pass_left.start()
    if weights_first:
        average_outer()
        t_copy(0).start()
        send_middle()
        t_copy(1).start()
    pass_right.wait()
    pass_left.wait()

    def choose(step):
        @pl.loop(0, 2)
        def _(i):
            places = lax.broadcasted_iota(jnp.int32, (1024, TILE), 0)
            wanted = ids[step : step + 1, pl.ds(pl.multiple_of(i * TILE, TILE), TILE)]
            picks = jnp.where(wanted == places, 1.0, 0.0).astype(jnp.bfloat16)
            chosen[pl.ds(pl.multiple_of(step * 512 + i * TILE, TILE), TILE), :] = transposed_dot(
                picks, pool_all[...]
            ).astype(jnp.bfloat16)

    choose(0)
    og_copies[0].wait()

    @pl.loop(0, 2)
    def _(c):
        t_copy(c).wait()

        if not ring and outer != 0 and not weights_first:
            @pl.when(c == 1)
            def _():
                average_outer()
                send_middle()

        @pl.loop(0, 2)
        def _(part):
            @pl.loop(0, 2)
            def _(i):
                at = pl.ds(pl.multiple_of(part * 512 + i * TILE, TILE), TILE)
                fresh = transposed_dot(og_all[0, :, at], chosen[pl.ds(0, 512), columns(c)])
                mixed = (
                    0.5
                    * (t_own[c, at, :].astype(jnp.float32) + t_in[c, at, :].astype(jnp.float32))
                    + fresh
                    - g_own[c, at, :].astype(jnp.float32)
                )
                y_all[0, c, at, :] = mixed.astype(jnp.bfloat16)
                delta[c, at, :] = fresh

            y_copy(c, part).start()

        if ring:
            @pl.when(c == 1)
            def _():
                average_quarter()

    choose(1)
    og_copies[1].wait()

    @each_tile
    def _(at):
        for c in range(2):
            fresh = transposed_dot(og_all[1, :, at], chosen[pl.ds(512, 512), columns(c)])
            delta[c, at, :] = fresh - delta[c, at, :]

    late = inner in (3, 4)

    @pl.loop(0, 3)
    def _(job):
        c = (job + 1) % 2

        if not ring and not late:
            @pl.when(job == 1)
            def _():
                average_inner()

        @pl.when(job > 0)
        def _():
            y_copy(c, 0).wait()
            y_copy(c, 1).wait()

            @each_tile
            def _(at):
                mixed = (
                    0.5
                    * (
                        y_all[0, c, at, :].astype(jnp.float32)
                        + y_all[1 + c, 0, at, :].astype(jnp.float32)
                    )
                    + delta[c, at, :]
                ).astype(jnp.bfloat16)
                y_all[1 + c, 1, at, :] = mixed
                new_t[at, columns(c)] = mixed

        def squares(i, totals):
            at = pl.ds(pl.multiple_of(i * TILE, TILE), TILE)
            out = []
            for k in range(2):
                values = y_all[job, k, at, :].astype(jnp.float32)
                out.append(totals[k] + jnp.sum(values * values, axis=0, keepdims=True))
            return tuple(out)

        totals = lax.fori_loop(0, 4, squares, (jnp.zeros((1, BLOCK), jnp.float32),) * 2)
        inverse = [
            1.0 / (jnp.sqrt(jnp.sum(total, axis=1, keepdims=True)) + 1e-07) for total in totals
        ]

        @each_tile
        def _(at):
            for k in range(2):
                x_ref[k, at, :] = (
                    y_all[job, k, at, :].astype(jnp.float32) * inverse[k]
                ).astype(jnp.bfloat16)

        @pl.loop(0, NS_ITERS)
        def _(turn):
            for k in range(2):
                x = x_ref[k]
                gram = transposed_dot(x, x).astype(jnp.bfloat16)
                square = jnp.dot(gram, gram, preferred_element_type=jnp.float32)
                poly[k] = (quintic_b * gram.astype(jnp.float32) + quintic_c * square).astype(
                    jnp.bfloat16
                )

            @each_tile
            def _(at):
                for k in range(2):
                    tile = x_ref[k, at, :]
                    x_ref[k, at, :] = (
                        quintic_a * tile.astype(jnp.float32)
                        + jnp.dot(tile, poly[k], preferred_element_type=jnp.float32)
                    ).astype(jnp.bfloat16)

        @pl.when(job == 0)
        def _():
            @each_tile
            def _(at):
                for k in range(2):
                    acc[k, at, :] = 0.5 * x_ref[k, at, :].astype(jnp.float32)

        @pl.when(job > 0)
        def _():
            @each_tile
            def _(at):
                acc[c, at, :] += 0.5 * x_ref[0, at, :].astype(jnp.float32) + x_ref[
                    1, at, :
                ].astype(jnp.float32)

    if ring:
        for j in range(3):
            quarter_out(j).wait()
    else:
        if late:
            average_inner()
        for copy in w_back:
            copy.wait()
    scale = 0.2 * math.sqrt(1024)

    @each_tile
    def _(at):
        for c in range(2):
            new_w[at, columns(c)] = (
                w_all[at, columns(c)].astype(jnp.float32) - scale * acc[c, at, :]
            ).astype(jnp.bfloat16)


COST = (0, 1, 2, 4, 1)


def both_steps(first, levels, ids, weights, tracker, grad_prev, pool, og):
    second = (first + 1) % levels
    outer, inner = (first, second) if COST[first] <= COST[second] else (second, first)
    ring = first == 2
    anywhere = pl.BlockSpec(memory_space=pl.ANY)
    vmem = pl.BlockSpec(memory_space=pltpu.VMEM)
    bf16, f32 = jnp.bfloat16, jnp.float32
    dma = pltpu.SemaphoreType.DMA
    return pl.pallas_call(
        functools.partial(kernel, first, second, outer, inner, ring),
        out_shape=(jax.ShapeDtypeStruct((1024, 1024), bf16),) * 2,
        in_specs=[vmem] + [anywhere] * 5,
        out_specs=(vmem, vmem),
        scratch_shapes=[
            pltpu.VMEM((2, 1024, BLOCK), bf16),
            pltpu.VMEM((2, 1024, BLOCK), bf16),
            pltpu.VMEM((2, 1024, BLOCK), bf16),
            pltpu.VMEM((3, 2, 1024, BLOCK), bf16),
            pltpu.VMEM((1024, 1024), bf16),
            pltpu.VMEM((2, 512, 1024), bf16),
            pltpu.VMEM((1024, 1024), bf16),
            pltpu.VMEM((2, 1024, BLOCK), f32),
            pltpu.VMEM((2, 1024, BLOCK), f32),
            pltpu.VMEM((2, 1024, BLOCK), bf16),
            pltpu.VMEM((2, BLOCK, BLOCK), bf16),
            pltpu.VMEM((256 if ring else 512, 1024), bf16),
            pltpu.VMEM((512, 1024), bf16),
            pltpu.VMEM((512, 1024), bf16),
            pltpu.VMEM((512, 1024), bf16),
            pltpu.VMEM((1024, 1024), bf16),
            pltpu.VMEM((3, 256, 1024), bf16),
            dma((8,)), dma((4,)), dma((4,)), dma((2,)), dma((2,)),
            dma((2,)), dma((2,)), dma((2, 2)), dma((2, 2)), dma((9,)), dma((9,)), dma((6,)), dma((6,)),
        ],
        compiler_params=pltpu.CompilerParams(
            collective_id=first, has_side_effects=True, vmem_limit_bytes=58 << 20
        ),
        name=f"steps_{first}",
    )(ids, weights, tracker, grad_prev, pool, og)


def body(weights, tracker, grad_prev, pool, out_grads, row_ids, step_index):
    levels = lax.axis_size("rep").bit_length() - 1
    branches = [functools.partial(both_steps, first, levels) for first in range(levels)]
    new_w, new_t = lax.switch(
        step_index[0] % levels,
        branches,
        row_ids[0],
        weights[0],
        tracker[0],
        grad_prev[0],
        pool[0],
        out_grads[0],
    )
    return (new_w[None], new_t[None])


def solution(mesh):
    in_specs = (
        P("rep", "row", "col"),
        P("rep", "row", "col"),
        P("rep", "row", "col"),
        P("rep", "row", "col"),
        P("rep", None, "col", "row"),
        P("rep", None, None),
        P(),
    )
    out_specs = (P("rep", "row", "col"), P("rep", "row", "col"))
    return jax.shard_map(body, mesh=mesh, in_specs=in_specs, out_specs=out_specs, check_vma=False)
```
